32 devices in a mesh: expert: 16 (over z, y, x), tensor: 2 (over core).
Axes of the slice: x: 2, y: 2, z: 4, core: 2. Of those that a mesh axis runs over, the one named last changes fastest.
Arguments:
- moe_in: bfloat16 [4096, 1536], P('expert', 'tensor'), may hold values from -6 to 6
- moe_grad: bfloat16 [4096, 1536], P('expert', 'tensor'), may hold values from -6 to 6
- routes: int32 [4096, 2], P('expert'), may hold values from 0 to 15, all different within a row; in each aligned block of 256 rows (0 to 255, 256 to 511, ...) at most 64 rows name the same one
- gates: float32 [4096, 2], P('expert'), may hold values from 0.25 to 1
- w_in: bfloat16 [16, 1536, 3072], P('expert', None, 'tensor'), may hold values from -0.15625 to 0.15625
- w_out: bfloat16 [16, 3072, 1536], P('expert', 'tensor'), may hold values from -0.109375 to 0.109375
- conv_in: bfloat16 [4096, 1536], P('expert', 'tensor'), may hold values from -6 to 6
- w_glu: bfloat16 [1536, 2, 1536], P(None, None, 'tensor'), may hold values from -0.15625 to 0.15625
- kernel: float32 [32, 1536], P(None, 'tensor'), may hold values from -1 to 1
- conv_grad: bfloat16 [4096, 1536], P('expert', 'tensor'), may hold values from -6 to 6
Outputs:
- moe_input_grad: bfloat16 [1536, 4096], P('tensor', 'expert')
- conv_input_grad: bfloat16 [1536, 4096], P('tensor', 'expert')
The draws below stay inside these ranges and needn't reach their ends.
Inputs may be any that keep to these rules, and one draw needn't show every extreme that they name: `routes`: each row names two different experts. Among the 256 frames of one index of the expert axis no expert is named by more than 64 of them, a bound that some block reaches.
All inputs are finite; a program needn't handle non-finite values.
Results may differ from the reference program's by a relative error of at most 0.0072.
Values may be sent and summed in bfloat16 or wider, within the bound.
No kernel may reach another device: no remote copies, remote signals or barrier semaphores. Data moves between devices by JAX's collectives and lax.ppermute only.
A program may use at most 128 MiB of HBM per device.

```python
import math
import jax
import jax.numpy as jnp
import numpy as np
from jax import lax

D = 1536
FF = 3072
KERNEL = 32
TOK_DEV = 256
EXPERTS = 16
CAP = 64
TOKENS = 4096
N_EXPERT = 16
N_TENSOR = 2


def shard_levels(rng, extent, cuts, smallest, top_value):
    def one(axis_at, parts):
        draws = jax.random.uniform(jax.random.fold_in(jax.random.fold_in(rng, 6), axis_at), (parts,), jnp.float32, smallest / len(cuts), top_value / len(cuts))
        return jnp.repeat(jnp.exp(draws), extent[axis_at] // parts).reshape((-1,) + (1,) * (len(extent) - axis_at - 1))

    gain = one(*cuts[0])
    for cut in cuts[1:]:
        gain = gain * one(*cut)
    return gain


def shared_out(rng, own, number, rows, amount, top, reach, slope):
    sequence = jax.random.permutation(rng, amount)
    packed, common = load_shares(amount, rows * top, reach, slope, True), load_shares(amount, rows * top, reach, slope, False)
    places = jnp.arange(amount)

    def named(lengths, offset_by):
        used = int((lengths > 0).sum())
        fixed = max(1, used // 4)
        passed = fixed + (places - fixed + offset_by * (used - fixed)) % max(1, amount - fixed)
        return jnp.zeros((amount,), jnp.int32).at[sequence[jnp.where(places < fixed, places, passed)]].set(jnp.asarray(lengths, jnp.int32))

    lengths = jnp.where(number % 4 == 0, named(packed, number // 4), named(common, number - number // 4 - 1))
    mixed = jax.random.permutation(jax.random.fold_in(own, 3), amount)
    giver, sink = mixed[0:amount // 2 * 2:2], mixed[1:amount // 2 * 2:2]
    room = jnp.minimum(lengths[giver] - 1, reach - lengths[sink]) // 2
    room = jnp.where((giver == sequence[0]) | (sink == sequence[0]) | (lengths[sink] == 0), 0, jnp.maximum(room, 0))
    passed = jax.random.randint(jax.random.fold_in(own, 4), (amount // 2,), 0, 1 << 20) % (room + 1)
    lengths = lengths.at[giver].add(-passed).at[sink].add(passed)
    items = jnp.searchsorted(jnp.cumsum(lengths), jnp.arange(rows * top), side="right").astype(jnp.int32)
    listing = items.reshape(top, rows).T
    listing = listing[jax.random.permutation(jax.random.fold_in(own, 1), rows)]
    offset_by = jax.random.randint(jax.random.fold_in(own, 2), (rows, 1), 0, top)
    return jnp.take_along_axis(listing, (jnp.arange(top)[None, :] + offset_by) % top, axis=1)


def load_shares(number_of, total, reach, skew, full):
    weights = [(1 << 20) // math.isqrt(rank ** skew) + 1 for rank in range(1, number_of + 1)]
    largest = reach if full else min(reach, max(-(-total // number_of), total * weights[0] // sum(weights)))
    least = 1 if total - largest >= number_of - 1 else 0
    counts, spare = [largest] + [least] * (number_of - 1), total - largest - least * (number_of - 1)
    while spare > 0:
        candidates = [i for i in range(1, number_of) if counts[i] < largest] or [i for i in range(1, number_of) if counts[i] < reach]
        whole, budget = sum([weights[i] for i in candidates]), spare
        for i in candidates:
            more = min(reach - counts[i], max(1, budget * weights[i] // whole), spare)
            counts[i] = counts[i] + more
            spare = spare - more
    return np.array(counts)


def scatter_about(rng, extent, spread, reach, pieces=(), held_as=jnp.bfloat16):
    entries = spread * jax.random.normal(rng, extent, jnp.float32)
    if pieces:
        entries = entries * shard_levels(rng, extent, pieces, -0.22, 0.18)
    return jnp.clip(entries, -reach, reach).astype(held_as)


def setup_inputs(seed: int = 0) -> dict:
    key_of = jax.random.split(jax.random.key(seed), 11)
    moe_in = scatter_about(key_of[0], (TOKENS, D), 1.0, 6.0, ((0, 16), (1, 2)))
    moe_grad = scatter_about(key_of[1], (TOKENS, D), 1.0, 6.0, ((0, 16), (1, 2)))
    routes_keys = jax.random.split(jax.random.fold_in(key_of[2], 1), TOKENS // TOK_DEV)
    routes_turns = jax.random.permutation(jax.random.fold_in(key_of[2], 3), TOKENS // TOK_DEV)
    routes = jax.vmap(lambda own, number: shared_out(jax.random.fold_in(key_of[2], 2), own, number, TOK_DEV, EXPERTS, 2, CAP, 2))(routes_keys, routes_turns).reshape((TOKENS, 2))
    gates = jnp.clip(0.25 + 0.75 * jax.random.uniform(key_of[3], (TOKENS, 2), jnp.float32) ** shard_levels(key_of[3], (TOKENS, 2), ((0, 16),), -0.2, 0.2), 0.25, 1.0)
    w_in = scatter_about(key_of[4], (EXPERTS, D, FF), D ** -0.5, 0.15625, ((0, 16), (2, 2)))
    w_out = scatter_about(key_of[5], (EXPERTS, FF, D), FF ** -0.5, 0.109375, ((0, 16), (1, 2)))
    conv_in = scatter_about(key_of[6], (TOKENS, D), 1.0, 6.0, ((0, 16), (1, 2)))
    w_glu = scatter_about(key_of[7], (D, 2, D), D ** -0.5, 0.15625, ((2, 2),))
    kernel = scatter_about(key_of[8], (KERNEL, D), KERNEL ** -0.5, 1.0, ((1, 2),), jnp.float32)
    conv_grad = scatter_about(key_of[9], (TOKENS, D), 1.0, 6.0, ((0, 16), (1, 2)))
    return dict(moe_in=moe_in, moe_grad=moe_grad, routes=routes, gates=gates, w_in=w_in, w_out=w_out, conv_in=conv_in, w_glu=w_glu, kernel=kernel, conv_grad=conv_grad)


def slot_table(routes):
    pairs = TOK_DEV * 2
    flat = routes.reshape(N_EXPERT, pairs)
    onehot = (flat[:, :, None] == jnp.arange(EXPERTS, dtype=jnp.int32)[None, None, :]).astype(jnp.int32)
    running = jnp.cumsum(onehot, axis=1)
    position = jnp.sum(onehot * running, axis=2) - 1
    device = jnp.arange(N_EXPERT, dtype=jnp.int32)[:, None]
    slot = (device * CAP + position).astype(jnp.int32)
    return flat.reshape(-1).astype(jnp.int32), slot.reshape(-1)


def reference(moe_in, moe_grad, routes, gates, w_in, w_out, conv_in, w_glu, kernel, conv_grad):
    expert_of, slot_of = slot_table(routes)
    total_pairs = 2 * TOKENS
    source = jnp.full((EXPERTS, N_EXPERT * CAP), total_pairs, jnp.int32)
    source = source.at[expert_of, slot_of].set(jnp.arange(total_pairs, dtype=jnp.int32))
    scaled = (moe_grad.astype(jnp.float32)[:, None, :] * gates[:, :, None]).astype(jnp.bfloat16)
    scaled = jnp.concatenate([scaled.reshape(total_pairs, D), jnp.zeros((1, D), jnp.bfloat16)], axis=0)
    inputs = jnp.concatenate([moe_in, jnp.zeros((1, D), jnp.bfloat16)], axis=0)
    hid_width = FF // N_TENSOR

    def expert_rows(index):
        rows = source[index]
        x_rows = inputs[rows // 2]
        g_rows = scaled[rows]
        win = w_in[index]
        wout = w_out[index]
        pre = jnp.dot(x_rows, win, preferred_element_type=jnp.float32)
        act_grad = lax.dot_general(g_rows, wout, (((1,), (1,)), ((), ())), preferred_element_type=jnp.float32)
        sig = jax.nn.sigmoid(pre)
        pre_grad = (act_grad * sig * (1.0 + pre * (1.0 - sig))).astype(jnp.bfloat16)
        total = jnp.zeros((N_EXPERT * CAP, D), jnp.float32)
        for block in range(N_TENSOR):
            part = lax.dot_general(pre_grad[:, block * hid_width:(block + 1) * hid_width],
                                   win[:, block * hid_width:(block + 1) * hid_width],
                                   (((1,), (1,)), ((), ())), preferred_element_type=jnp.float32)
            total = total + lax.optimization_barrier(part.astype(jnp.bfloat16)).astype(jnp.float32)
        return total.astype(jnp.bfloat16)

    slot_grads = lax.map(expert_rows, jnp.arange(EXPERTS, dtype=jnp.int32))
    picked = slot_grads[expert_of, slot_of].astype(jnp.float32).reshape(TOKENS, 2, D)
    moe_input_grad = jnp.sum(picked, axis=1).astype(jnp.bfloat16).T

    glu_pre = jnp.dot(conv_in, w_glu.reshape(D, 2 * D), preferred_element_type=jnp.float32).reshape(TOKENS, 2, D)
    value = glu_pre[:, 0]
    gate = glu_pre[:, 1]
    grads = conv_grad.astype(jnp.float32)
    grads = jnp.pad(grads, ((0, KERNEL - 1), (0, 0)))
    mix_grad = jnp.zeros((TOKENS, D), jnp.float32)
    for offset in range(KERNEL):
        mix_grad = mix_grad + kernel[offset] * grads[offset:offset + TOKENS]
    sig_gate = jax.nn.sigmoid(gate)
    glu_grad = jnp.stack([mix_grad * sig_gate, mix_grad * value * sig_gate * (1.0 - sig_gate)], axis=1).astype(jnp.bfloat16)
    ch_width = D // N_TENSOR
    conv_total = jnp.zeros((D, TOKENS), jnp.float32)
    for block in range(N_TENSOR):
        grad_block = glu_grad[:, :, block * ch_width:(block + 1) * ch_width].reshape(TOKENS, 2 * ch_width)
        weight_block = w_glu[:, :, block * ch_width:(block + 1) * ch_width].reshape(D, 2 * ch_width)
        part = lax.dot_general(weight_block, grad_block, (((1,), (1,)), ((), ())), preferred_element_type=jnp.float32)
        conv_total = conv_total + lax.optimization_barrier(part.astype(jnp.bfloat16)).astype(jnp.float32)
    conv_input_grad = conv_total.astype(jnp.bfloat16)
    return moe_input_grad, conv_input_grad
```

```python
import jax
import jax.numpy as jnp
from jax import lax
from jax.experimental import pallas as pl
from jax.experimental.pallas import tpu as pltpu
from jax.sharding import PartitionSpec as P

BF = jnp.bfloat16
F32 = jnp.float32


def swap(x):
    return lax.ppermute(x, "tensor", [(0, 1), (1, 0)])


def gather_channels(x):
    if lax.axis_size("tensor") != 2:
        return lax.all_gather(x, "tensor", axis=1, tiled=True)
    other = swap(x)
    first = lax.axis_index("tensor") == 0
    return jnp.concatenate([jnp.where(first, x, other), jnp.where(first, other, x)], axis=1)


def scatter_sum(term, axis):
    if lax.axis_size("tensor") != 2:
        return lax.psum_scatter(term, "tensor", scatter_dimension=axis, tiled=True)
    first = lax.axis_index("tensor") == 0
    low, high = jnp.split(term, 2, axis=axis)
    other = swap(jnp.where(first, high, low))
    own = jnp.where(first, low, high)
    return (own.astype(F32) + other.astype(F32)).astype(BF)


def slot_of(routes_t, frames, first, number):
    experts = first + lax.broadcasted_iota(jnp.int32, (number, frames), 0)
    named = (routes_t[0:1] == experts) | (routes_t[1:2] == experts)
    before = lax.broadcasted_iota(jnp.int32, (frames, frames), 0) < lax.broadcasted_iota(
        jnp.int32, (frames, frames), 1
    )
    count = jnp.dot(named.astype(BF), before.astype(BF), preferred_element_type=F32)
    return jnp.where(named, count.astype(jnp.int32), -1), experts


def one_hot(slot, capacity):
    number, frames = slot.shape
    place = lax.broadcasted_iota(jnp.int32, (number, capacity, frames), 1)
    return (slot[:, None, :] == place).reshape(number * capacity, frames)


def dispatch_kernel(base_ref, r_ref, g_ref, in_ref, grad_ref, out_ref):
    number, twice, channels = out_ref.shape
    capacity = twice // 2
    frames = r_ref.shape[1]
    experts = base_ref[0] + lax.broadcasted_iota(jnp.int32, (number, frames), 0)
    one = r_ref[0:1, :] == experts
    two = r_ref[1:2, :] == experts
    named = jnp.where(one, 1.0, jnp.where(two, 1.0, 0.0))
    before = lax.broadcasted_iota(jnp.int32, (frames, frames), 0) < lax.broadcasted_iota(
        jnp.int32, (frames, frames), 1
    )
    count = jnp.dot(named.astype(BF), jnp.where(before, 1.0, 0.0).astype(BF), preferred_element_type=F32)
    slot = jnp.where(named > 0.0, count.astype(jnp.int32), -1)
    gate = jnp.where(one, g_ref[0:1, :], g_ref[1:2, :])
    place = lax.broadcasted_iota(jnp.int32, (number, capacity, frames), 1)
    hot = jnp.broadcast_to(slot[:, None, :], place.shape) == place
    scale = jnp.sum(jnp.where(hot, jnp.broadcast_to(gate[:, None, :], place.shape), 0.0), axis=2, keepdims=True)
    hot = jnp.where(hot, 1.0, 0.0).reshape(number * capacity, frames).astype(BF)
    x = jnp.dot(hot, in_ref[...], preferred_element_type=F32).astype(BF)
    g = jnp.dot(hot, grad_ref[...], preferred_element_type=F32).reshape(number, capacity, channels) * scale
    out_ref[:, :capacity, :] = x.reshape(number, capacity, channels)
    out_ref[:, capacity:, :] = g.astype(BF)


def dispatch(base, number, capacity, r, g, in_rows, grad_rows):
    frames, channels = in_rows.shape
    vmem = pl.BlockSpec(memory_space=pltpu.VMEM)
    flops = 4 * number * capacity * frames * channels
    return pl.pallas_call(
        dispatch_kernel,
        out_shape=jax.ShapeDtypeStruct((number, 2 * capacity, channels), BF),
        in_specs=[pl.BlockSpec(memory_space=pltpu.SMEM)] + [vmem] * 4,
        out_specs=vmem,
        cost_estimate=pl.CostEstimate(
            flops=flops, bytes_accessed=4 * channels * (frames + number * capacity), transcendentals=0
        ),
        compiler_params=pltpu.CompilerParams(vmem_limit_bytes=16 << 20),
        name="dispatch",
    )(base.reshape(1), r, g, in_rows, grad_rows)


def finish_kernel(place_ref, here_ref, back_ref, *rest):
    rest[-1][...] = (here_ref[...].astype(F32) + back_ref[...].astype(F32)).astype(BF)


def finish(place, here, back, others):
    rows, channels = here.shape
    extra = [] if others is None else [others]
    steps = 2
    return pl.pallas_call(
        finish_kernel,
        out_shape=jax.ShapeDtypeStruct((2 * rows, channels), BF),
        grid_spec=pltpu.PrefetchScalarGridSpec(
            num_scalar_prefetch=1,
            grid=(steps,),
            in_specs=[pl.BlockSpec((rows // steps, channels), lambda i, place: (i, 0))] * 2
            + [pl.BlockSpec(memory_space=pl.ANY)] * len(extra),
            out_specs=pl.BlockSpec((rows // steps, channels), lambda i, place: (place[0] * steps + i, 0)),
        ),
        input_output_aliases={3: 0} if extra else {},
        cost_estimate=pl.CostEstimate(
            flops=rows * channels, bytes_accessed=6 * rows * channels, transcendentals=0
        ),
        compiler_params=pltpu.CompilerParams(vmem_limit_bytes=8 << 20),
        name="finish",
    )(place.reshape(1), here, back, *extra)


def body(moe_in, moe_grad, routes, gates, w_in, w_out, conv_in, w_glu, kernel, conv_grad):
    frames, channels = moe_in.shape
    sources = lax.axis_size("expert")
    half = sources // 2
    capacity = 4 * frames // sources
    rows = half * capacity
    model = w_in.shape[1]
    w_in, w_out = w_in[0], w_out[0]
    me = lax.axis_index("expert")
    base = me & half
    halves = [list(range(half)), list(range(half, sources))]
    mirror = [(i, i ^ half) for i in range(sources)]

    def in_half(rows):
        return lax.all_to_all(
            rows, "expert", split_axis=0, concat_axis=0, tiled=True, axis_index_groups=halves
        )

    far_routes = lax.ppermute(routes, "expert", mirror).T
    far_gates = lax.ppermute(gates, "expert", mirror).T
    routes_t, gates_t = routes.T, gates.T
    far_in = lax.ppermute(moe_in, "expert", mirror)
    far_grad = lax.ppermute(moe_grad, "expert", mirror)

    both = dispatch(base, half, capacity, routes_t, gates_t, moe_in, moe_grad)
    near_rows = in_half(both).reshape(half, 2, capacity, channels)
    both = dispatch(base, half, capacity, far_routes, far_gates, far_in, far_grad)
    far_rows = in_half(both).reshape(half, 2, capacity, channels)

    def hidden(first, second):
        sig = jax.nn.sigmoid(first)
        return (second * sig * (1.0 + first * (1.0 - sig))).astype(BF)

    def times(a, w, over):
        return lax.dot_general(a, w, (((1,), (over,)), ((), ())), preferred_element_type=F32)

    if lax.axis_size("tensor") == 2:
        core = lax.axis_index("tensor")
        own, oth = core * channels, (1 - core) * channels
        in_own = lax.dynamic_slice_in_dim(w_in, own, channels, 0)
        in_oth = lax.dynamic_slice_in_dim(w_in, oth, channels, 0)
        out_own = lax.dynamic_slice_in_dim(w_out, own, channels, 1)
        out_oth = lax.dynamic_slice_in_dim(w_out, oth, channels, 1)

    near_at = base // half

    def expert(pairs, place, others):
        if lax.axis_size("tensor") != 2:
            x = gather_channels(pairs[:, 0].reshape(rows, channels))
            g = gather_channels(pairs[:, 1].reshape(rows, channels))
            pre_grad = hidden(times(x, w_in, 0), times(g, w_out, 1))
            part = scatter_sum(times(pre_grad, w_in, 1).astype(BF), 1)
            others = jnp.zeros((2 * rows, channels), BF) if others is None else others
            return lax.dynamic_update_slice_in_dim(others, part, place * rows, 0)
        other = swap(pairs)
        first = times(pairs[:, 0].reshape(rows, channels), in_own, 0)
        second = times(pairs[:, 1].reshape(rows, channels), out_own, 1)
        first = first + times(other[:, 0].reshape(rows, channels), in_oth, 0)
        second = second + times(other[:, 1].reshape(rows, channels), out_oth, 1)
        pre_grad = hidden(first, second)
        away = times(pre_grad, in_oth, 1).astype(BF)
        back = swap(away)
        here = times(pre_grad, in_own, 1).astype(BF)
        return finish(place, here, back, others)

    slot_grads = expert(near_rows, near_at, None)
    slot_grads = expert(far_rows, 1 - near_at, slot_grads)

    returned = lax.all_to_all(
        slot_grads.reshape(sources, capacity, channels), "expert", split_axis=0, concat_axis=0, tiled=True
    ).reshape(sources * capacity, channels)
    slot_all, _ = slot_of(routes_t, frames, 0, sources)
    hot_all = one_hot(slot_all, capacity)
    moe_input_grad = lax.dot_general(
        returned, hot_all.astype(BF), (((0,), (0,)), ((), ())), preferred_element_type=F32
    ).astype(BF)

    conv_wide = gather_channels(conv_in)
    glu_weight = w_glu.reshape(model, 2 * channels)
    glu_pre = jnp.dot(conv_wide, glu_weight, preferred_element_type=F32)
    taps = kernel.shape[0]
    future = lax.ppermute(conv_grad[: taps - 1], "expert", [(i, i - 1) for i in range(1, sources)])
    extended = jnp.concatenate([conv_grad, future], axis=0).astype(F32)
    mix_grad = jnp.zeros((frames, channels), F32)
    for offset in range(taps):
        mix_grad = mix_grad + kernel[offset] * extended[offset : offset + frames]
    value = glu_pre[:, :channels]
    gate = glu_pre[:, channels:]
    sig_gate = jax.nn.sigmoid(gate)
    glu_grad = jnp.concatenate([mix_grad * sig_gate, mix_grad * value * sig_gate * (1.0 - sig_gate)], axis=1).astype(BF)
    term = lax.dot_general(
        glu_weight, glu_grad, (((1,), (1,)), ((), ())), preferred_element_type=F32
    ).astype(BF)
    conv_input_grad = scatter_sum(term, 0)
    return (moe_input_grad, conv_input_grad)


def solution(mesh):
    placed = (
        P("expert", "tensor"),
        P("expert", "tensor"),
        P("expert", None),
        P("expert", None),
        P("expert", None, "tensor"),
        P("expert", "tensor", None),
        P("expert", "tensor"),
        P(None, None, "tensor"),
        P(None, "tensor"),
        P("expert", "tensor"),
    )

    return jax.shard_map(
        body,
        mesh=mesh,
        in_specs=placed,
        out_specs=(P("tensor", "expert"), P("tensor", "expert")),
        check_vma=False,
    )
```

```python
import math
import jax
import jax.numpy as jnp
from jax import lax
from jax.experimental import pallas as pl
from jax.experimental.pallas import tpu as pltpu
from jax.sharding import PartitionSpec as P

BF = jnp.bfloat16
F32 = jnp.float32


def swap(x):
    return lax.ppermute(x, "tensor", [(0, 1), (1, 0)])


def gather_channels(x):
    if lax.axis_size("tensor") != 2:
        return lax.all_gather(x, "tensor", axis=1, tiled=True)
    other = swap(x)
    first = lax.axis_index("tensor") == 0
    return jnp.concatenate([jnp.where(first, x, other), jnp.where(first, other, x)], axis=1)


def scatter_sum(term, axis):
    if lax.axis_size("tensor") != 2:
        return lax.psum_scatter(term, "tensor", scatter_dimension=axis, tiled=True)
    first = lax.axis_index("tensor") == 0
    low, high = jnp.split(term, 2, axis=axis)
    other = swap(jnp.where(first, high, low))
    own = jnp.where(first, low, high)
    return (own.astype(F32) + other.astype(F32)).astype(BF)


def slots(r_ref_0, r_ref_1, experts):
    frames = experts.shape[1]
    one = r_ref_0 == experts
    named = jnp.where(one, 1.0, jnp.where(r_ref_1 == experts, 1.0, 0.0))
    before = lax.broadcasted_iota(jnp.int32, (frames, frames), 0) < lax.broadcasted_iota(
        jnp.int32, (frames, frames), 1
    )
    count = jnp.dot(named.astype(BF), jnp.where(before, 1.0, 0.0).astype(BF), preferred_element_type=F32)
    return jnp.where(named > 0.0, count.astype(jnp.int32), -1), one


def dispatch_kernel(origin_ref, r_ref, g_ref, in_ref, grad_ref, *outs):
    capacity, twice = outs[0].shape[-2:]
    channels = twice // 2
    number = len(outs) if len(outs) > 1 else outs[0].shape[0]
    frames = r_ref.shape[1]
    experts = origin_ref[0] ^ lax.broadcasted_iota(jnp.int32, (number, frames), 0)
    slot, one = slots(r_ref[0:1, :], r_ref[1:2, :], experts)
    gate = jnp.where(one, g_ref[0:1, :], g_ref[1:2, :])
    place = lax.broadcasted_iota(jnp.int32, (number, capacity, frames), 1)
    hot = jnp.broadcast_to(slot[:, None, :], place.shape) == place
    scale = jnp.sum(jnp.where(hot, jnp.broadcast_to(gate[:, None, :], place.shape), 0.0), axis=2, keepdims=True)
    hot = jnp.where(hot, 1.0, 0.0).reshape(number * capacity, frames).astype(BF)
    x = jnp.dot(hot, in_ref[...], preferred_element_type=F32).astype(BF).reshape(number, capacity, channels)
    g = jnp.dot(hot, grad_ref[...], preferred_element_type=F32).reshape(number, capacity, channels) * scale
    g = g.astype(BF)
    if len(outs) == 1:
        outs[0][:, :, :channels] = x
        outs[0][:, :, channels:] = g
    else:
        for i, out in enumerate(outs):
            out[:, :channels] = x[i]
            out[:, channels:] = g[i]


def dispatch(origin, number, capacity, r, g, in_rows, grad_rows, apart):
    frames, channels = in_rows.shape
    flops = 4 * number * capacity * frames * channels
    if apart:
        shape = (jax.ShapeDtypeStruct((capacity, 2 * channels), BF),) * number
        outs = [pl.BlockSpec((capacity, 2 * channels), lambda i: (0, 0))] * number
    else:
        shape = jax.ShapeDtypeStruct((number, capacity, 2 * channels), BF)
        outs = pl.BlockSpec(shape.shape, lambda i: (0, 0, 0))
    return pl.pallas_call(
        dispatch_kernel,
        grid=(1,),
        out_shape=shape,
        in_specs=[pl.BlockSpec(memory_space=pltpu.SMEM)]
        + [pl.BlockSpec(a.shape, lambda i: (0, 0)) for a in (r, g, in_rows, grad_rows)],
        out_specs=outs,
        cost_estimate=pl.CostEstimate(
            flops=flops, bytes_accessed=(64 if apart else 4) * channels * (frames + number * capacity), transcendentals=0
        ),
        compiler_params=pltpu.CompilerParams(vmem_limit_bytes=(16 if apart else 60) << 20),
        name="dispatch",
    )(origin.reshape(1), r, g, in_rows, grad_rows)


def gradient(first, second):
    sig = jax.nn.sigmoid(first)
    return (second * sig * (1.0 + first * (1.0 - sig))).astype(BF)


def times(a, w, over):
    return lax.dot_general(a, w, (((1,), (over,)), ((), ())), preferred_element_type=F32)


def warm_kernel(in_ref, out_ref, done_ref):
    done_ref[...] = jnp.zeros_like(done_ref)


def warm(w_in, w_out):
    return pl.pallas_call(
        warm_kernel,
        out_shape=jax.ShapeDtypeStruct((8, 128), F32),
        in_specs=[pl.BlockSpec(memory_space=pltpu.VMEM)] * 2,
        out_specs=pl.BlockSpec(memory_space=pltpu.VMEM),
        cost_estimate=pl.CostEstimate(flops=0, bytes_accessed=4096, transcendentals=0),
        compiler_params=pltpu.CompilerParams(vmem_limit_bytes=1 << 20),
        name="warm",
    )(w_in, w_out)


def expert_kernel(core_ref, own_ref, oth_ref, in_ref, out_ref, here_ref, away_ref, hidden):
    channels = own_ref.shape[1] // 2
    width = in_ref.shape[1]
    chunk = math.gcd(width, 512)
    piece = math.gcd(channels, 256)
    own = pl.multiple_of(core_ref[0] * channels, channels)
    oth = pl.multiple_of((1 - core_ref[0]) * channels, channels)
    for at in range(0, width, chunk):
        part = slice(at, at + chunk)
        one = times(own_ref[:, :channels], in_ref[pl.ds(own, channels), part], 0)
        one += times(oth_ref[:, :channels], in_ref[pl.ds(oth, channels), part], 0)
        two = times(own_ref[:, channels:], out_ref[part, pl.ds(own, channels)], 1)
        two += times(oth_ref[:, channels:], out_ref[part, pl.ds(oth, channels)], 1)
        hidden[:, part] = gradient(one, two)
    for ref, begin in ((away_ref, oth), (here_ref, own)):
        for at in range(0, channels, piece):
            rows = pl.ds(pl.multiple_of(begin + at, piece), piece)
            ref[:, at : at + piece] = times(hidden[...], in_ref[rows, :], 1).astype(BF)


def expert(core, own, oth, w_in, w_out):
    rows, channels = own.shape[0], own.shape[1] // 2
    width = w_in.shape[1]
    whole = pl.BlockSpec((rows, 2 * channels), lambda i: (0, 0))
    out = pl.BlockSpec((rows, channels), lambda i: (0, 0))
    shape = jax.ShapeDtypeStruct((rows, channels), BF)
    return pl.pallas_call(
        expert_kernel,
        grid=(1,),
        out_shape=(shape, shape),
        in_specs=[pl.BlockSpec(memory_space=pltpu.SMEM), whole, whole]
        + [pl.BlockSpec(memory_space=pltpu.VMEM)] * 2,
        out_specs=(out, out),
        scratch_shapes=[pltpu.VMEM((rows, width), BF)],
        cost_estimate=pl.CostEstimate(
            flops=12 * rows * channels * width,
            bytes_accessed=8 * width * channels + 12 * rows * channels,
            transcendentals=rows * width,
        ),
        compiler_params=pltpu.CompilerParams(vmem_limit_bytes=rows * (8 * width + 24 * channels) + (1 << 20)),
        name="expert",
    )(core.reshape(1), own, oth, w_in, w_out)


def finish_kernel(here_ref, back_ref, *outs):
    capacity = outs[0].shape[0]
    for i, out in enumerate(outs):
        part = slice(i * capacity, (i + 1) * capacity)
        out[...] = (here_ref[part].astype(F32) + back_ref[part].astype(F32)).astype(BF)


def finish(here, back, pieces):
    rows, channels = here.shape
    capacity = rows // pieces
    whole = pl.BlockSpec((rows, channels), lambda i: (0, 0))
    return pl.pallas_call(
        finish_kernel,
        grid=(1,),
        out_shape=(jax.ShapeDtypeStruct((capacity, channels), BF),) * pieces,
        in_specs=[whole] * 2,
        out_specs=[pl.BlockSpec((capacity, channels), lambda i: (0, 0))] * pieces,
        cost_estimate=pl.CostEstimate(
            flops=rows * channels, bytes_accessed=96 * rows * channels, transcendentals=0
        ),
        compiler_params=pltpu.CompilerParams(vmem_limit_bytes=16 * rows * channels),
        name="finish",
    )(here, back)


def join_kernel(*refs):
    capacity = refs[0].shape[0]
    for i in range(refs[-1].shape[0] // capacity):
        ref = refs[i]
        refs[-1][i * capacity : (i + 1) * capacity, :] = ref[...]


def join(parts, after=None):
    capacity, width = parts[0].shape
    rows = capacity * len(parts)
    extra = [] if after is None else [after]
    return pl.pallas_call(
        join_kernel,
        grid=(1,),
        out_shape=jax.ShapeDtypeStruct((rows, width), BF),
        in_specs=[pl.BlockSpec((capacity, width), lambda i: (0, 0))] * len(parts)
        + [pl.BlockSpec(a.shape, lambda i: (0, 0)) for a in extra],
        out_specs=pl.BlockSpec((rows, width), lambda i: (0, 0)),
        cost_estimate=pl.CostEstimate(flops=0, bytes_accessed=4 * rows * width, transcendentals=0),
        compiler_params=pltpu.CompilerParams(vmem_limit_bytes=8 << 20),
        name="join",
    )(*parts, *extra)


def combine_kernel(slot_ref, near_ref, *refs):
    out_ref, far = refs[-2:]
    capacity = refs[0].shape[0]
    number, frames = slot_ref.shape
    for i, ref in enumerate(refs[:-2]):
        far[i * capacity : (i + 1) * capacity, :] = ref[...]
    place = lax.broadcasted_iota(jnp.int32, (number, capacity, frames), 1)
    hot = jnp.broadcast_to(slot_ref[...][:, None, :], place.shape) == place
    hot = jnp.where(hot, 1.0, 0.0).reshape(number * capacity, frames).astype(BF)
    half = number * capacity // 2

    def gathered(rows, picks):
        return lax.dot_general(rows, picks, (((0,), (0,)), ((), ())), preferred_element_type=F32)

    out_ref[...] = (gathered(near_ref[...], hot[:half]) + gathered(far[...], hot[half:])).astype(BF)


def combine(slot, near, parts):
    _, frames = slot.shape
    rows, channels = near.shape
    return pl.pallas_call(
        combine_kernel,
        grid=(1,),
        out_shape=jax.ShapeDtypeStruct((channels, frames), BF),
        in_specs=[pl.BlockSpec(a.shape, lambda i: (0, 0)) for a in (slot, near, *parts)],
        out_specs=pl.BlockSpec((channels, frames), lambda i: (0, 0)),
        scratch_shapes=[pltpu.VMEM((rows, channels), BF)],
        cost_estimate=pl.CostEstimate(
            flops=4 * rows * channels * frames, bytes_accessed=6 * rows * channels, transcendentals=0
        ),
        compiler_params=pltpu.CompilerParams(vmem_limit_bytes=12 << 20),
        name="combine",
    )(slot, near, *parts)


def body(moe_in, moe_grad, routes, gates, w_in, w_out, conv_in, w_glu, kernel, conv_grad):
    frames, channels = moe_in.shape
    sources = lax.axis_size("expert")
    half = sources // 2
    quarter = half // 2
    capacity = 4 * frames // sources
    model = w_in.shape[1]
    w_in, w_out = w_in[0], w_out[0]
    me = lax.axis_index("expert")
    base = me & half
    halves = [list(range(half)), list(range(half, sources))]

    def flip(x, by):
        return lax.ppermute(x, "expert", [(i, i ^ by) for i in range(sources)])

    def in_half(rows):
        return lax.all_to_all(
            rows, "expert", split_axis=0, concat_axis=0, tiled=True, axis_index_groups=halves
        )

    far_routes = flip(routes, half).T
    far_gates = flip(gates, half).T
    routes_t, gates_t = routes.T, gates.T
    far_in = flip(moe_in, half)
    far_grad = flip(moe_grad, half)

    both = dispatch(base, half, capacity, routes_t, gates_t, moe_in, moe_grad, False)
    near_rows = in_half(both).reshape(half * capacity, 2 * channels)
    sent = dispatch(me, half, capacity, far_routes, far_gates, far_in, far_grad, True)
    arrived = [sent[0]]
    for k in range(1, half):
        arrived.append(flip(sent[k], k))

    def share(own, pieces):
        if lax.axis_size("tensor") != 2:
            x = gather_channels(own[:, :channels])
            g = gather_channels(own[:, channels:])
            pre_grad = gradient(times(x, w_in, 0), times(g, w_out, 1))
            part = scatter_sum(times(pre_grad, w_in, 1).astype(BF), 1)
            return jnp.split(part, pieces, axis=0)
        core = lax.axis_index("tensor")
        oth = swap(own)
        here, away = expert(core, own, oth, w_in, w_out)
        back = swap(away)
        return finish(here, back, pieces)

    ready = warm(w_in, w_out)
    plane = join(arrived[:quarter], ready)
    beyond = join(arrived[quarter:])
    far_grads = list(share(plane, quarter))
    (near_grads,) = share(near_rows, 1)
    far_grads += list(share(beyond, half - quarter))

    returned = [in_half(near_grads.reshape(half, capacity, channels)).reshape(half * capacity, channels)]
    for k in range(half):
        returned.append(flip(far_grads[k], half ^ k))
    order = lax.broadcasted_iota(jnp.int32, (sources, frames), 0)
    experts = jnp.where(order < half, base, me) ^ order
    slot, _ = slots(routes_t[0:1], routes_t[1:2], experts)
    moe_input_grad = combine(slot, returned[0], returned[1:])

    conv_wide = gather_channels(conv_in)
    glu_weight = w_glu.reshape(model, 2 * channels)
    glu_pre = jnp.dot(conv_wide, glu_weight, preferred_element_type=F32)
    taps = kernel.shape[0]
    future = lax.ppermute(conv_grad[: taps - 1], "expert", [(i, i - 1) for i in range(1, sources)])
    extended = jnp.concatenate([conv_grad, future], axis=0).astype(F32)
    mix_grad = jnp.zeros((frames, channels), F32)
    for offset in range(taps):
        mix_grad = mix_grad + kernel[offset] * extended[offset : offset + frames]
    value = glu_pre[:, :channels]
    gate = glu_pre[:, channels:]
    sig_gate = jax.nn.sigmoid(gate)
    glu_grad = jnp.concatenate([mix_grad * sig_gate, mix_grad * value * sig_gate * (1.0 - sig_gate)], axis=1).astype(BF)
    term = lax.dot_general(
        glu_weight, glu_grad, (((1,), (1,)), ((), ())), preferred_element_type=F32
    ).astype(BF)
    conv_input_grad = scatter_sum(term, 0)
    return (moe_input_grad, conv_input_grad)


def solution(mesh):
    placed = (
        P("expert", "tensor"),
        P("expert", "tensor"),
        P("expert", None),
        P("expert", None),
        P("expert", None, "tensor"),
        P("expert", "tensor", None),
        P("expert", "tensor"),
        P(None, None, "tensor"),
        P(None, "tensor"),
        P("expert", "tensor"),
    )

    return jax.shard_map(
        body,
        mesh=mesh,
        in_specs=placed,
        out_specs=(P("tensor", "expert"), P("tensor", "expert")),
        check_vma=False,
    )
```

```python
import math
import jax
import jax.numpy as jnp
from jax import lax
from jax.experimental import pallas as pl
from jax.experimental.pallas import tpu as pltpu
from jax.sharding import PartitionSpec as P

BF = jnp.bfloat16
F32 = jnp.float32


def swap(x):
    return lax.ppermute(x, "tensor", [(0, 1), (1, 0)])


def gather_channels(x):
    if lax.axis_size("tensor") != 2:
        return lax.all_gather(x, "tensor", axis=1, tiled=True)
    other = swap(x)
    first = lax.axis_index("tensor") == 0
    return jnp.concatenate([jnp.where(first, x, other), jnp.where(first, other, x)], axis=1)


def scatter_sum(term, axis):
    if lax.axis_size("tensor") != 2:
        return lax.psum_scatter(term, "tensor", scatter_dimension=axis, tiled=True)
    first = lax.axis_index("tensor") == 0
    low, high = jnp.split(term, 2, axis=axis)
    other = swap(jnp.where(first, high, low))
    own = jnp.where(first, low, high)
    return (own.astype(F32) + other.astype(F32)).astype(BF)


def slots(r_ref_0, r_ref_1, experts):
    frames = experts.shape[1]
    one = r_ref_0 == experts
    named = jnp.where(one, 1.0, jnp.where(r_ref_1 == experts, 1.0, 0.0))
    before = lax.broadcasted_iota(jnp.int32, (frames, frames), 0) < lax.broadcasted_iota(
        jnp.int32, (frames, frames), 1
    )
    count = jnp.dot(named.astype(BF), jnp.where(before, 1.0, 0.0).astype(BF), preferred_element_type=F32)
    return jnp.where(named > 0.0, count.astype(jnp.int32), -1), one


def dispatch_kernel(origin_ref, r_ref, g_ref, in_ref, grad_ref, *outs):
    capacity, twice = outs[0].shape[-2:]
    channels = twice // 2
    number = len(outs) if len(outs) > 1 else outs[0].shape[0]
    frames = r_ref.shape[1]
    experts = origin_ref[0] ^ lax.broadcasted_iota(jnp.int32, (number, frames), 0)
    slot, one = slots(r_ref[0:1, :], r_ref[1:2, :], experts)
    gate = jnp.where(one, g_ref[0:1, :], g_ref[1:2, :])
    place = lax.broadcasted_iota(jnp.int32, (number, capacity, frames), 1)
    hot = jnp.broadcast_to(slot[:, None, :], place.shape) == place
    scale = jnp.sum(jnp.where(hot, jnp.broadcast_to(gate[:, None, :], place.shape), 0.0), axis=2, keepdims=True)
    hot = jnp.where(hot, 1.0, 0.0).reshape(number * capacity, frames).astype(BF)
    x = jnp.dot(hot, in_ref[...], preferred_element_type=F32).astype(BF).reshape(number, capacity, channels)
    g = jnp.dot(hot, grad_ref[...], preferred_element_type=F32).reshape(number, capacity, channels) * scale
    g = g.astype(BF)
    if len(outs) == 1:
        outs[0][:, :, :channels] = x
        outs[0][:, :, channels:] = g
    else:
        for i, out in enumerate(outs):
            out[:, :channels] = x[i]
            out[:, channels:] = g[i]


def dispatch(origin, number, capacity, r, g, in_rows, grad_rows, apart):
    frames, channels = in_rows.shape
    flops = 4 * number * capacity * frames * channels
    if apart:
        shape = (jax.ShapeDtypeStruct((capacity, 2 * channels), BF),) * number
        outs = [pl.BlockSpec((capacity, 2 * channels), lambda i: (0, 0))] * number
    else:
        shape = jax.ShapeDtypeStruct((number, capacity, 2 * channels), BF)
        outs = pl.BlockSpec(shape.shape, lambda i: (0, 0, 0))
    return pl.pallas_call(
        dispatch_kernel,
        grid=(1,),
        out_shape=shape,
        in_specs=[pl.BlockSpec(memory_space=pltpu.SMEM)]
        + [pl.BlockSpec(a.shape, lambda i: (0, 0)) for a in (r, g, in_rows, grad_rows)],
        out_specs=outs,
        cost_estimate=pl.CostEstimate(
            flops=flops, bytes_accessed=(64 if apart else 4) * channels * (frames + number * capacity), transcendentals=0
        ),
        compiler_params=pltpu.CompilerParams(vmem_limit_bytes=(16 if apart else 60) << 20),
        name="dispatch",
    )(origin.reshape(1), r, g, in_rows, grad_rows)


def gradient(first, second):
    sig = jax.nn.sigmoid(first)
    return (second * sig * (1.0 + first * (1.0 - sig))).astype(BF)


def times(a, w, over):
    return lax.dot_general(a, w, (((1,), (over,)), ((), ())), preferred_element_type=F32)


def expert_kernel(core_ref, own_ref, oth_ref, in_ref, out_ref, here_ref, away_ref, hidden, *held):
    channels = own_ref.shape[1] // 2
    width = in_ref.shape[1]
    chunk = math.gcd(width, 512)
    piece = math.gcd(channels, 256)
    own = pl.multiple_of(core_ref[0] * channels, channels)
    oth = pl.multiple_of((1 - core_ref[0]) * channels, channels)
    here_in, here_out, sems = held if held else (in_ref, out_ref, None)
    copies = []
    for i, at in enumerate(range(0, width, chunk)):
        part = pl.ds(at, chunk)
        if held:
            copies.append(pltpu.make_async_copy(in_ref.at[:, part], here_in.at[:, part], sems.at[0, i]))
            copies[-1].start()
            copies.append(pltpu.make_async_copy(out_ref.at[part, :], here_out.at[part, :], sems.at[1, i]))
            copies[-1].start()
    copies = iter(copies)
    for at in range(0, width, chunk):
        part = slice(at, at + chunk)
        if held:
            next(copies).wait()
        one = times(own_ref[:, :channels], here_in[pl.ds(own, channels), part], 0)
        one += times(oth_ref[:, :channels], here_in[pl.ds(oth, channels), part], 0)
        if held:
            next(copies).wait()
        two = times(own_ref[:, channels:], here_out[part, pl.ds(own, channels)], 1)
        two += times(oth_ref[:, channels:], here_out[part, pl.ds(oth, channels)], 1)
        hidden[:, part] = gradient(one, two)
    for ref, begin in ((away_ref, oth), (here_ref, own)):
        for at in range(0, channels, piece):
            rows = pl.ds(pl.multiple_of(begin + at, piece), piece)
            ref[:, at : at + piece] = times(hidden[...], here_in[rows, :], 1).astype(BF)


def expert(core, own, oth, w_in, w_out, fetch):
    rows, channels = own.shape[0], own.shape[1] // 2
    width = w_in.shape[1]
    whole = pl.BlockSpec((rows, 2 * channels), lambda i: (0, 0))
    out = pl.BlockSpec((rows, channels), lambda i: (0, 0))
    shape = jax.ShapeDtypeStruct((rows, channels), BF)
    weight = pl.BlockSpec(memory_space=pltpu.HBM if fetch else pltpu.VMEM)
    held = [pltpu.VMEM(w.shape, BF) for w in (w_in, w_out)] + [
        pltpu.SemaphoreType.DMA((2, width // math.gcd(width, 512)))
    ]
    return pl.pallas_call(
        expert_kernel,
        grid=(1,),
        out_shape=(shape, shape),
        in_specs=[pl.BlockSpec(memory_space=pltpu.SMEM), whole, whole, weight, weight],
        out_specs=(out, out),
        scratch_shapes=[pltpu.VMEM((rows, width), BF)] + (held if fetch else []),
        cost_estimate=pl.CostEstimate(
            flops=12 * rows * channels * width,
            bytes_accessed=8 * width * channels + 12 * rows * channels,
            transcendentals=rows * width,
        ),
        compiler_params=pltpu.CompilerParams(
            vmem_limit_bytes=rows * (8 * width + 24 * channels) + ((11 if rows > 256 else 1) << 20)
        ),
        name="expert",
    )(core.reshape(1), own, oth, w_in, w_out)


def finish_kernel(here_ref, back_ref, *outs):
    capacity = outs[0].shape[0]
    for i, out in enumerate(outs):
        part = slice(i * capacity, (i + 1) * capacity)
        out[...] = (here_ref[part].astype(F32) + back_ref[part].astype(F32)).astype(BF)


def finish(here, back, pieces):
    rows, channels = here.shape
    capacity = rows // pieces
    whole = pl.BlockSpec((rows, channels), lambda i: (0, 0))
    return pl.pallas_call(
        finish_kernel,
        grid=(1,),
        out_shape=(jax.ShapeDtypeStruct((capacity, channels), BF),) * pieces,
        in_specs=[whole] * 2,
        out_specs=[pl.BlockSpec((capacity, channels), lambda i: (0, 0))] * pieces,
        cost_estimate=pl.CostEstimate(
            flops=rows * channels, bytes_accessed=96 * rows * channels, transcendentals=0
        ),
        compiler_params=pltpu.CompilerParams(vmem_limit_bytes=16 * rows * channels),
        name="finish",
    )(here, back)


def join_kernel(*refs):
    capacity = refs[0].shape[0]
    for i in range(refs[-1].shape[0] // capacity):
        ref = refs[i]
        refs[-1][i * capacity : (i + 1) * capacity, :] = ref[...]


def join(parts, after=None):
    capacity, width = parts[0].shape
    rows = capacity * len(parts)
    extra = [] if after is None else [after]
    return pl.pallas_call(
        join_kernel,
        grid=(1,),
        out_shape=jax.ShapeDtypeStruct((rows, width), BF),
        in_specs=[pl.BlockSpec((capacity, width), lambda i: (0, 0))] * len(parts)
        + [pl.BlockSpec(a.shape, lambda i: (0, 0)) for a in extra],
        out_specs=pl.BlockSpec((rows, width), lambda i: (0, 0)),
        cost_estimate=pl.CostEstimate(flops=0, bytes_accessed=4 * rows * width, transcendentals=0),
        compiler_params=pltpu.CompilerParams(vmem_limit_bytes=8 << 20),
        name="join",
    )(*parts, *extra)


def combine_kernel(slot_ref, near_ref, *refs):
    out_ref, far = refs[-2:]
    capacity = refs[0].shape[0]
    number, frames = slot_ref.shape
    for i, ref in enumerate(refs[:-2]):
        far[i * capacity : (i + 1) * capacity, :] = ref[...]
    place = lax.broadcasted_iota(jnp.int32, (number, capacity, frames), 1)
    hot = jnp.broadcast_to(slot_ref[...][:, None, :], place.shape) == place
    hot = jnp.where(hot, 1.0, 0.0).reshape(number * capacity, frames).astype(BF)
    half = number * capacity // 2

    def gathered(rows, picks):
        return lax.dot_general(rows, picks, (((0,), (0,)), ((), ())), preferred_element_type=F32)

    out_ref[...] = (gathered(near_ref[...], hot[:half]) + gathered(far[...], hot[half:])).astype(BF)


def combine(slot, near, parts):
    _, frames = slot.shape
    rows, channels = near.shape
    return pl.pallas_call(
        combine_kernel,
        grid=(1,),
        out_shape=jax.ShapeDtypeStruct((channels, frames), BF),
        in_specs=[pl.BlockSpec(a.shape, lambda i: (0, 0)) for a in (slot, near, *parts)],
        out_specs=pl.BlockSpec((channels, frames), lambda i: (0, 0)),
        scratch_shapes=[pltpu.VMEM((rows, channels), BF)],
        cost_estimate=pl.CostEstimate(
            flops=4 * rows * channels * frames, bytes_accessed=6 * rows * channels, transcendentals=0
        ),
        compiler_params=pltpu.CompilerParams(vmem_limit_bytes=12 << 20),
        name="combine",
    )(slot, near, *parts)


def body(moe_in, moe_grad, routes, gates, w_in, w_out, conv_in, w_glu, kernel, conv_grad):
    frames, channels = moe_in.shape
    sources = lax.axis_size("expert")
    half = sources // 2
    quarter = half // 2
    capacity = 4 * frames // sources
    model = w_in.shape[1]
    w_in, w_out = w_in[0], w_out[0]
    me = lax.axis_index("expert")
    base = me & half
    halves = [list(range(half)), list(range(half, sources))]

    def flip(x, by):
        return lax.ppermute(x, "expert", [(i, i ^ by) for i in range(sources)])

    def in_half(rows):
        return lax.all_to_all(
            rows, "expert", split_axis=0, concat_axis=0, tiled=True, axis_index_groups=halves
        )

    far_routes = flip(routes, half).T
    far_gates = flip(gates, half).T
    routes_t, gates_t = routes.T, gates.T
    far_in = flip(moe_in, half)
    far_grad = flip(moe_grad, half)

    both = dispatch(base, half, capacity, routes_t, gates_t, moe_in, moe_grad, False)
    near_rows = in_half(both).reshape(half * capacity, 2 * channels)
    sent = dispatch(me, half, capacity, far_routes, far_gates, far_in, far_grad, True)
    arrived = [sent[0]]
    for k in range(1, half):
        arrived.append(flip(sent[k], k))

    def share(own, pieces):
        if lax.axis_size("tensor") != 2:
            x = gather_channels(own[:, :channels])
            g = gather_channels(own[:, channels:])
            pre_grad = gradient(times(x, w_in, 0), times(g, w_out, 1))
            part = scatter_sum(times(pre_grad, w_in, 1).astype(BF), 1)
            return jnp.split(part, pieces, axis=0)
        core = lax.axis_index("tensor")
        oth = swap(own)
        here, away = expert(core, own, oth, w_in, w_out, False)
        back = swap(away)
        return finish(here, back, pieces)

    plane = join(arrived[:quarter])
    beyond = join(arrived[quarter:])
    far_grads = list(share(plane, quarter))
    (near_grads,) = share(near_rows, 1)
    far_grads += list(share(beyond, half - quarter))

    returned = [in_half(near_grads.reshape(half, capacity, channels)).reshape(half * capacity, channels)]
    for k in range(half):
        returned.append(flip(far_grads[k], half ^ k))
    order = lax.broadcasted_iota(jnp.int32, (sources, frames), 0)
    experts = jnp.where(order < half, base, me) ^ order
    slot, _ = slots(routes_t[0:1], routes_t[1:2], experts)
    moe_input_grad = combine(slot, returned[0], returned[1:])

    conv_wide = gather_channels(conv_in)
    glu_weight = w_glu.reshape(model, 2 * channels)
    glu_pre = jnp.dot(conv_wide, glu_weight, preferred_element_type=F32)
    taps = kernel.shape[0]
    future = lax.ppermute(conv_grad[: taps - 1], "expert", [(i, i - 1) for i in range(1, sources)])
    extended = jnp.concatenate([conv_grad, future], axis=0).astype(F32)
    mix_grad = jnp.zeros((frames, channels), F32)
    for offset in range(taps):
        mix_grad = mix_grad + kernel[offset] * extended[offset : offset + frames]
    value = glu_pre[:, :channels]
    gate = glu_pre[:, channels:]
    sig_gate = jax.nn.sigmoid(gate)
    glu_grad = jnp.concatenate([mix_grad * sig_gate, mix_grad * value * sig_gate * (1.0 - sig_gate)], axis=1).astype(BF)
    term = lax.dot_general(
        glu_weight, glu_grad, (((1,), (1,)), ((), ())), preferred_element_type=F32
    ).astype(BF)
    conv_input_grad = scatter_sum(term, 0)
    return (moe_input_grad, conv_input_grad)


def solution(mesh):
    placed = (
        P("expert", "tensor"),
        P("expert", "tensor"),
        P("expert", None),
        P("expert", None),
        P("expert", None, "tensor"),
        P("expert", "tensor", None),
        P("expert", "tensor"),
        P(None, None, "tensor"),
        P(None, "tensor"),
        P("expert", "tensor"),
    )

    return jax.shard_map(
        body,
        mesh=mesh,
        in_specs=placed,
        out_specs=(P("tensor", "expert"), P("tensor", "expert")),
        check_vma=False,
    )
```
